32 devices in a mesh: replica: 4 (over y, x), fsdp: 2 (over core), tensor: 4 (over z).
Axes of the slice: x: 2, y: 2, z: 4, core: 2. Of those that a mesh axis runs over, the one named last changes fastest.
Arguments:
- attn_out: bfloat16 [2048, 8192], P(('replica', 'tensor'), 'fsdp'), may hold values from -6 to 6
- out_grad: bfloat16 [2048, 8192], P(('replica', 'fsdp'), 'tensor'), may hold values from -0.25 to 0.25
- error_in: float32 [4, 8192, 8192], P('replica', 'fsdp', 'tensor'), may hold values from -4 to 4
- factor_in: float32 [8192, 32], P('tensor'), may hold values from -0.0625 to 0.0625
Outputs:
- new_error: float32 [4, 8192, 8192], P('replica', 'fsdp', 'tensor')
- update: bfloat16 [8192, 8192], P('fsdp', 'tensor')
- new_factor: float32 [8192, 32], P('tensor')
The draws below stay inside these ranges and needn't reach their ends.
All inputs are finite; a program needn't handle non-finite values.
Results may differ from the reference program's by a relative error of at most 0.001.
Values may be sent and summed in bfloat16 or wider, within the bound.
A program may use at most 128 MiB of HBM per device.

```python
import jax
import jax.numpy as jnp
from jax import lax

DIN = 8192
DOUT = 8192
RANK = 32
TOK = 512
TOK_ALL = 2048
N_REPLICA = 4


def shard_levels(own_key, shape, cuts, least, high):
    factor_of, own = 1.0, jax.random.fold_in(own_key, 6)
    for axis_at, parts in cuts:
        steps = jnp.exp(jax.random.uniform(jax.random.fold_in(own, axis_at), (parts,), jnp.float32, least / len(cuts), high / len(cuts)))
        factor_of = factor_of * jnp.repeat(steps, shape[axis_at] // parts).reshape([-1 if axis == axis_at else 1 for axis in range(len(shape))])
    return factor_of


def centred(rng, extent, deviation, reach, cuts=(), kind=jnp.bfloat16):
    drawn = jax.random.normal(rng, extent, jnp.float32) * deviation
    if len(cuts) > 0:
        drawn = shard_levels(rng, extent, cuts, -0.22, 0.18) * drawn
    return jnp.clip(drawn, min=-reach, max=reach).astype(kind)


def setup_inputs(seed: int = 0) -> dict:
    arg_keys = jax.random.split(jax.random.key(seed), 5)
    return {
        "attn_out": centred(arg_keys[0], (TOK_ALL, DIN), 1.0, 6.0, ((0, 16), (1, 2))),
        "out_grad": centred(arg_keys[1], (TOK_ALL, DOUT), TOK ** -0.5, 0.25, ((0, 8), (1, 4))),
        "error_in": centred(arg_keys[2], (N_REPLICA, DIN, DOUT), 0.5, 4.0, ((0, 4), (1, 2), (2, 4)), jnp.float32),
        "factor_in": centred(arg_keys[3], (DOUT, RANK), DOUT ** -0.5, 0.0625, ((0, 4),), jnp.float32),
    }


def reference(attn_out, out_grad, error_in, factor_in):
    tokens = attn_out.shape[0] // N_REPLICA
    activations = attn_out.reshape(N_REPLICA, tokens, DIN)
    cotangents = out_grad.reshape(N_REPLICA, tokens, DOUT)

    def per_replica(items):
        act_block, cot_block, memory = items
        return jnp.dot(act_block.T.astype(jnp.float32), cot_block.astype(jnp.float32), preferred_element_type=jnp.float32) + memory
    merged = lax.map(per_replica, (activations, cotangents, error_in))
    left = jnp.einsum('rij,jk->ik', merged, factor_in, precision=lax.Precision.HIGHEST) / N_REPLICA
    gram_matrix = jnp.dot(left.T, left, precision=lax.Precision.HIGHEST)
    triangle = jnp.linalg.cholesky(gram_matrix)
    orthonormal = jax.scipy.linalg.solve_triangular(triangle, left.T, lower=True).T
    new_factor = jnp.einsum('rij,ik->jk', merged, orthonormal, precision=lax.Precision.HIGHEST) / N_REPLICA
    decompressed = jnp.dot(orthonormal, new_factor.T, precision=lax.Precision.HIGHEST)
    new_error = merged - decompressed[None]
    return (new_error, decompressed.astype(jnp.bfloat16), new_factor)
```

```python
import functools

import jax
import jax.numpy as jnp
from jax import lax
from jax.experimental import pallas as pl
from jax.experimental.pallas import tpu as pltpu
from jax.sharding import PartitionSpec as P

MESH = pl.DeviceIdType.MESH
HIGHEST = lax.Precision.HIGHEST
F32, BF16 = jnp.float32, jnp.bfloat16
LANE = 128
NN = (((1,), (0,)), ((), ()))
NT = (((1,), (1,)), ((), ()))
TN = (((0,), (0,)), ((), ()))
VMEM_BYTES = 20 * 1024 * 1024
PIECES, LAG = 16, 2


def mul(a, b, dims=NN, precision=None):
    return lax.dot_general(a, b, dims, precision=precision, preferred_element_type=F32)


def split(x):
    high = x.astype(BF16)
    return high, (x - high.astype(F32)).astype(BF16)


def stacked(x):
    return jnp.concatenate(split(x), axis=0)


def folded(x):
    half = x.shape[0] // 2
    return x[:half] + x[half:]


class Cut:
    def __init__(self, rows, columns, pieces):
        self.down = 1
        while (columns * self.down) % (pieces * LANE) != 0:
            self.down *= 2
        self.across = pieces // self.down
        self.rows, self.columns = rows // self.down, columns // self.across

    def at(self, piece, start=0):
        row = pl.multiple_of((piece // self.across) * self.rows, 8)
        column = pl.multiple_of(start + (piece % self.across) * self.columns, LANE)
        return pl.ds(row, self.rows), pl.ds(column, self.columns)


def inverse_factor(gram):
    rank = gram.shape[0]
    row_at = lax.broadcasted_iota(jnp.int32, (rank, LANE), 0)
    lane_at = lax.broadcasted_iota(jnp.int32, (rank, LANE), 1)
    table = gram + jnp.where(lane_at == row_at + LANE // 2, 1.0, 0.0).astype(F32)
    for k in range(rank):
        row = table[k : k + 1, :]
        inverse = 1.0 / jnp.sqrt(row[:, k : k + 1])
        row = row * inverse
        column = jnp.where(row_at > k, table[:, k : k + 1] * inverse, 0.0)
        table = jnp.where(row_at == k, jnp.broadcast_to(row, table.shape), table - column * row)
    return table[:, LANE // 2 : LANE // 2 + rank]


def front(
    sizes,
    a_ref, g_ref, f_ref, e_ref,
    q_ref, n_ref, nt_ref, e_mem, a_all, g_all,
    f_mem, part, left, got_rep, mid, got_ten, gf_out, gf_slots, gram_slots, al_out, al_slots,
    n_part, n_got, n_full,
    e_sem, own_sem, out_sem, near_sem, ring_sem, g_sem, gf_sem, rep_sem, ten_sem, ten_back, rep_back, gram_sem, al_sem, n_sem, n_back,
):
    reps, fs, ts = sizes
    r, f, t = lax.axis_index("replica"), lax.axis_index("fsdp"), lax.axis_index("tensor")
    rank, rows = part.shape
    block = rows // reps
    tile = min(256, block)
    per = block // tile
    tok_g, tok_a = g_ref.shape[0], a_ref.shape[0]

    def row_copy(step):
        q = lax.rem(r + 1 + step // per, reps)
        at = pl.ds(pl.multiple_of(q * block + (step % per) * tile, tile), tile)
        return pltpu.make_async_copy(e_ref.at[at], e_mem.at[at], e_sem.at[step])

    for step in range(reps * per):
        row_copy(step).start()

    plane = [(df, dt) for df in range(fs) for dt in range(ts) if df + dt > 0]
    sheet = [(dr, df) for dr in range(reps) for df in range(fs) if dr + df > 0]

    def in_plane(df, dt):
        return {"replica": r, "fsdp": lax.rem(f + df, fs), "tensor": lax.rem(t + dt, ts)}

    def in_sheet(dr, df):
        return {"replica": lax.rem(r + dr, reps), "fsdp": lax.rem(f + df, fs), "tensor": t}

    barrier = pltpu.get_barrier_semaphore()
    greeted = [in_plane(*d) for d in plane] + [in_sheet(*d) for d in sheet if d[0] > 0]
    for device in greeted:
        pl.semaphore_signal(barrier, inc=1, device_id=device, device_id_type=MESH)

    high, low = split(f_ref[...])
    wide = jnp.concatenate(
        [high.astype(F32), low.astype(F32), jnp.zeros((LANE - 2 * rank, f_ref.shape[1]), F32)], axis=0
    )
    f_mem[...] = wide.T.astype(BF16)

    me_plane = f * ts + t
    chunk, a_parts, g_parts = gf_out.shape[2], al_out.shape[0], gf_out.shape[0]

    def meets(f_at, t_at):
        return (t_at // g_parts == f_at) if a_parts == 1 else (f_at // a_parts == t_at)

    gf = folded(mul(g_ref[...], f_mem[...]).T[: 2 * rank])
    for j in range(g_parts):
        gf_out[j] = gf[:, j * chunk : (j + 1) * chunk]

    @pl.when(meets(f, t))
    def _():
        gf_slots[me_plane] = gf_out[lax.rem(t, g_parts)]

    pl.semaphore_wait(barrier, len(greeted))

    def spread(source, slots, sems, goes, comes):
        copies = []
        for i, (df, dt) in enumerate(plane):
            to_f, to_t = lax.rem(f + df, fs), lax.rem(t + dt, ts)
            from_f, from_t = lax.rem(f + fs - df, fs), lax.rem(t + ts - dt, ts)
            copy = pltpu.make_async_remote_copy(
                src_ref=source(to_f, to_t), dst_ref=slots.at[me_plane],
                send_sem=sems.at[0, i], recv_sem=sems.at[1, i],
                device_id=in_plane(df, dt), device_id_type=MESH,
            )
            sends = goes(to_f, to_t)
            pl.when(sends)(copy.start)
            copies.append((copy, sends, comes(from_f, from_t)))
        return copies

    def settle(copies):
        for copy, sends, receives in copies:
            pl.when(receives)(copy.wait_recv)
            pl.when(sends)(copy.wait_send)

    gf_copies = spread(
        lambda to_f, to_t: gf_out.at[lax.rem(to_t, g_parts)], gf_slots, gf_sem,
        lambda to_f, to_t: meets(f, to_t), lambda from_f, from_t: meets(from_f, t),
    )

    g_own = pl.ds(pl.multiple_of(f * tok_g, tok_g), tok_g)
    a_own = pl.ds(pl.multiple_of(t * tok_a, tok_a), tok_a)
    own_copies = [
        pltpu.make_async_copy(a_ref, a_all.at[a_own], own_sem.at[0]),
        pltpu.make_async_copy(g_ref, g_all.at[g_own], own_sem.at[1]),
    ]
    for copy in own_copies:
        copy.start()
    g_copies = []
    for df in range(1, fs):
        copy = pltpu.make_async_remote_copy(
            src_ref=g_ref, dst_ref=g_all.at[g_own],
            send_sem=g_sem.at[0, df - 1], recv_sem=g_sem.at[1, df - 1],
            device_id=in_plane(df, 0), device_id_type=MESH,
        )
        copy.start()
        g_copies.append(copy)

    width = max(LANE, rows // PIECES)
    pieces = rows // width

    def part_of(block_at, p):
        return (
            pl.ds(pl.multiple_of(lax.rem(block_at + ts, ts) * tok_a, tok_a), tok_a),
            pl.ds(p * width, width),
        )

    def whole_of(block_at):
        return (pl.ds(pl.multiple_of(lax.rem(block_at + ts, ts) * tok_a, tok_a), tok_a), pl.ds(0, rows))

    def inside(x):
        return jnp.logical_and(x >= 0, x < ts)

    def lands_at(way, d, p):
        return ring_sem.at[way, p] if d == 2 else near_sem.at[way, d - 1]

    def bulk(way, d, p):
        sign = 1 - 2 * way
        block_at = t if d <= 2 else t - sign * (d - 1)
        dest = t + sign * (d if d <= 2 else 1)
        at = part_of(block_at, p)
        copy = pltpu.make_async_remote_copy(
            src_ref=a_ref.at[:, at[1]] if d <= 2 else a_all.at[at], dst_ref=a_all.at[at],
            send_sem=out_sem.at[way, d - 1], recv_sem=lands_at(way, d, p),
            device_id={"replica": r, "fsdp": f, "tensor": lax.rem(dest + ts, ts)},
            device_id_type=MESH,
        )
        return copy, jnp.logical_and(inside(block_at), inside(dest))

    def send(d, p):
        if d >= ts:
            return
        for way in range(2):
            copy, valid = bulk(way, d, p)
            pl.when(valid)(copy.start)

    def came(way, d, at, sem):
        copy = pltpu.make_async_remote_copy(
            src_ref=a_all.at[at], dst_ref=a_all.at[at], send_sem=out_sem.at[way, d - 1], recv_sem=sem,
            device_id=in_plane(0, 1), device_id_type=MESH,
        )
        pl.when(inside(t - (1 - 2 * way) * d))(copy.wait_recv)

    landed = set()

    def land(d, p):
        if (d, p) in landed:
            return
        landed.add((d, p))
        for way in range(2):
            came(way, d, part_of(t - (1 - 2 * way) * d, p), lands_at(way, d, p))

    def land_whole(d):
        if d == 2:
            for p in range(pieces):
                land(2, p)
        elif (d, -1) not in landed:
            landed.add((d, -1))
            for way in range(2):
                came(way, d, whole_of(t - (1 - 2 * way) * d), near_sem.at[way, d - 1])

    def pass_on(p):
        if ts > 3 and 0 <= p < pieces:
            land(2, p)
            send(3, p)

    turns = []
    for p in range(pieces + LAG):
        turns.append(((2, p), p - LAG))
        turns.append(((1, p), -1))

    def inject(count):
        for _ in range(min(count, len(turns))):
            (d, p), behind = turns.pop(0)
            if p < pieces:
                send(d, p)
            pass_on(behind)

    inject(2)

    rep_copies = []
    for dr in range(1, reps + 1):
        q = lax.rem(r + dr, reps)
        base = pl.multiple_of(q * block, LANE)
        inject(2)

        def tile_left(j, _, dr=dr, base=base):
            row_copy((dr - 1) * per + j).wait()
            at = pl.ds(pl.multiple_of(base + j * tile, tile), tile)
            eh, el = split(e_mem[at, :])
            total = mul(eh, f_mem[...]) + mul(el, f_mem[...])
            part[:, at] = folded(total.T[: 2 * rank])
            return 0

        lax.fori_loop(0, per, tile_left, 0)
        if dr == 1:
            settle(gf_copies)
            first = (t * tok_a) // tok_g
            totals = []
            for j in range(a_parts):
                total = gf_slots[(first + j) * ts]
                for dt in range(1, ts):
                    total = total + gf_slots[(first + j) * ts + dt]
                totals.append(total)
            own = stacked(jnp.concatenate(totals, axis=1))
        at = pl.ds(base, block)
        part[:, at] += folded(mul(own, a_ref[:, at]))
        if dr < reps:
            copy = pltpu.make_async_remote_copy(
                src_ref=part.at[:, at], dst_ref=got_rep.at[dr - 1],
                send_sem=rep_sem.at[0, dr - 1], recv_sem=rep_sem.at[1, dr - 1],
                device_id=in_sheet(dr, 0), device_id_type=MESH,
            )
            copy.start()
            rep_copies.append(copy)

    mine = pl.ds(pl.multiple_of(r * block, LANE), block)
    total = part[:, mine]
    for i, copy in enumerate(rep_copies):
        copy.wait()
        total = total + got_rep[i]
    mid[...] = total

    cut = Cut(rank, block, ts)
    ten_copies = []
    for dt in range(1, ts):
        copy = pltpu.make_async_remote_copy(
            src_ref=mid.at[cut.at(lax.rem(t + dt, ts))], dst_ref=got_ten.at[dt - 1],
            send_sem=ten_sem.at[0, dt - 1], recv_sem=ten_sem.at[1, dt - 1],
            device_id=in_plane(0, dt), device_id_type=MESH,
        )
        copy.start()
        ten_copies.append(copy)
    inject(1)
    total = mid[cut.at(t)]
    for i, copy in enumerate(ten_copies):
        copy.wait()
        total = total + got_ten[i]
    own = cut.at(t, r * block)
    left[own] = total * (1.0 / reps)
    back = []
    for dt in range(1, ts):
        copy = pltpu.make_async_remote_copy(
            src_ref=left.at[own], dst_ref=left.at[own],
            send_sem=ten_back.at[0, dt - 1], recv_sem=ten_back.at[1, dt - 1],
            device_id=in_plane(0, dt), device_id_type=MESH,
        )
        copy.start()
        back.append(copy)
    inject(1)
    for copy in back:
        copy.wait()
    back = []
    for dr in range(1, reps):
        copy = pltpu.make_async_remote_copy(
            src_ref=left.at[:, mine], dst_ref=left.at[:, mine],
            send_sem=rep_back.at[0, dr - 1], recv_sem=rep_back.at[1, dr - 1],
            device_id=in_sheet(dr, 0), device_id_type=MESH,
        )
        copy.start()
        back.append(copy)
    inject(3)
    for copy in back:
        copy.wait()

    whole = left[...]
    al = folded(mul(stacked(whole), a_ref[...], NT))
    for j in range(a_parts):
        al_out[j] = al[:, j * chunk : (j + 1) * chunk]

    @pl.when(meets(f, t))
    def _():
        al_slots[me_plane] = al_out[lax.rem(f, a_parts)]

    al_copies = spread(
        lambda to_f, to_t: al_out.at[lax.rem(to_f, a_parts)], al_slots, al_sem,
        lambda to_f, to_t: meets(to_f, t), lambda from_f, from_t: meets(f, from_t),
    )
    inject(4)
    gram_slots[f, :, 0:rank] = mul(whole, whole, NT, HIGHEST)
    gram_slots[f, :, rank:LANE] = jnp.zeros((rank, LANE - rank), F32)
    gram_copies = []
    for df in range(1, fs):
        copy = pltpu.make_async_remote_copy(
            src_ref=gram_slots.at[f], dst_ref=gram_slots.at[f],
            send_sem=gram_sem.at[0, df - 1], recv_sem=gram_sem.at[1, df - 1],
            device_id=in_plane(df, 0), device_id_type=MESH,
        )
        copy.start()
        gram_copies.append(copy)

    n_part[...] = jnp.zeros(n_part.shape, F32)

    def tile_right(j, _):
        at = pl.ds(pl.multiple_of(j * tile, tile), tile)
        eh, el = split(e_mem[at, :])
        both = stacked(left[:, at])
        n_part[...] += folded(mul(both, eh)) + mul(both[:rank], el)
        return 0

    lax.fori_loop(0, rows // tile, tile_right, 0)

    settle(al_copies)
    first = (f * tok_g) // tok_a
    totals = []
    for j in range(g_parts):
        total = al_slots[first + j]
        for df in range(1, fs):
            total = total + al_slots[df * ts + first + j]
        totals.append(total)
    tokens = stacked(jnp.concatenate(totals, axis=1))
    n_part[...] += folded(mul(tokens, g_ref[...]))

    n_cut = Cut(rank, n_part.shape[1], reps * fs)
    n_copies = []
    for i, (dr, df) in enumerate(sheet):
        owner = lax.rem(r + dr, reps) * fs + lax.rem(f + df, fs)
        copy = pltpu.make_async_remote_copy(
            src_ref=n_part.at[n_cut.at(owner)], dst_ref=n_got.at[i],
            send_sem=n_sem.at[0, i], recv_sem=n_sem.at[1, i],
            device_id=in_sheet(dr, df), device_id_type=MESH,
        )
        copy.start()
        n_copies.append(copy)

    inject(2)
    for copy in gram_copies:
        copy.wait()
    gram = gram_slots[0]
    for df in range(1, fs):
        gram = gram + gram_slots[df]
    inverse = inverse_factor(gram)
    high, low = split(mul(inverse, left[...], precision=HIGHEST))
    q_ref[0:rank] = high
    q_ref[rank : 2 * rank] = low
    q_ref[2 * rank :] = high

    place = n_cut.at(r * fs + f)
    total = n_part[place]
    for i, copy in enumerate(n_copies):
        copy.wait()
        total = total + n_got[i]
    n_full[place] = total * (1.0 / reps)
    back = []
    for i, (dr, df) in enumerate(sheet):
        copy = pltpu.make_async_remote_copy(
            src_ref=n_full.at[place], dst_ref=n_full.at[place],
            send_sem=n_back.at[0, i], recv_sem=n_back.at[1, i],
            device_id=in_sheet(dr, df), device_id_type=MESH,
        )
        copy.start()
        back.append(copy)
    inject(2)
    for copy in back:
        copy.wait()
    factor = mul(inverse, n_full[...], precision=HIGHEST)
    n_ref[...] = factor
    high, low = split(factor)
    nt_ref[0:rank] = high
    nt_ref[rank : 2 * rank] = high
    nt_ref[2 * rank :] = low

    inject(len(turns))
    for copy in own_copies + g_copies:
        copy.wait()
    for d in range(4, ts):
        land_whole(d - 1)
        for p in range(pieces):
            send(d, p)
    for d in range(1, ts):
        land_whole(d)
        for way in range(2):
            sign = 1 - 2 * way
            source = t if d <= 2 else t - sign * (d - 1)
            target = t + sign * (d if d <= 2 else 1)
            at = whole_of(t - sign * d)
            copy = pltpu.make_async_remote_copy(
                src_ref=a_all.at[at], dst_ref=a_all.at[at],
                send_sem=out_sem.at[way, d - 1], recv_sem=near_sem.at[way, d - 1],
                device_id=in_plane(0, 1), device_id_type=MESH,
            )
            pl.when(jnp.logical_and(inside(source), inside(target)))(copy.wait_send)


def run_front(sizes, a, g, f, e):
    reps, fs, ts = sizes
    rank, rows, columns = f.shape[0], e.shape[0], e.shape[1]
    tok_g, tok_a = g.shape[0], a.shape[0]
    block, chunk = rows // reps, min(tok_a, tok_g)
    cut, n_cut = Cut(rank, block, ts), Cut(rank, columns, reps * fs)
    tiles = rows // min(256, block)
    plane, sheet = fs * ts - 1, reps * fs - 1
    vmem = pl.BlockSpec(memory_space=pltpu.VMEM)
    dma = pltpu.SemaphoreType.DMA
    return pl.pallas_call(
        functools.partial(front, sizes),
        out_shape=(
            jax.ShapeDtypeStruct((3 * rank, rows), BF16),
            jax.ShapeDtypeStruct((rank, columns), F32),
            jax.ShapeDtypeStruct((3 * rank, columns), BF16),
            pltpu.VMEM((rows, columns), F32),
            pltpu.VMEM((tok_a * ts, rows), BF16),
            pltpu.VMEM((tok_g * fs, columns), BF16),
        ),
        in_specs=[vmem, vmem, vmem, pl.BlockSpec(memory_space=pl.ANY)],
        out_specs=(vmem,) * 6,
        scratch_shapes=[
            pltpu.VMEM((columns, LANE), BF16),
            pltpu.VMEM((rank, rows), F32),
            pltpu.VMEM((rank, rows), F32),
            pltpu.VMEM((reps - 1, rank, block), F32),
            pltpu.VMEM((rank, block), F32),
            pltpu.VMEM((ts - 1, cut.rows, cut.columns), F32),
            pltpu.VMEM((tok_g // chunk, rank, chunk), F32),
            pltpu.VMEM((fs * ts, rank, chunk), F32),
            pltpu.VMEM((fs, rank, LANE), F32),
            pltpu.VMEM((tok_a // chunk, rank, chunk), F32),
            pltpu.VMEM((fs * ts, rank, chunk), F32),
            pltpu.VMEM((rank, columns), F32),
            pltpu.VMEM((sheet, n_cut.rows, n_cut.columns), F32),
            pltpu.VMEM((rank, columns), F32),
            dma((tiles,)), dma((2,)), dma((2, ts)), dma((2, ts)), dma((2, PIECES)), dma((2, fs)), dma((2, plane)), dma((2, reps - 1)), dma((2, ts - 1)), dma((2, ts - 1)),
            dma((2, reps - 1)), dma((2, fs)), dma((2, plane)), dma((2, sheet)), dma((2, sheet)),
        ],
        compiler_params=pltpu.CompilerParams(
            collective_id=0, has_side_effects=True, vmem_limit_bytes=VMEM_BYTES
        ),
        cost_estimate=pl.CostEstimate(
            flops=100_000_000_000, bytes_accessed=rows * columns * 8, transcendentals=0
        ),
        name="front",
    )(a, g, f, e)


def finish(a_ref, g_ref, e_ref, q_ref, n_ref, error_ref, update_ref):
    tile = error_ref.shape[0]
    at = pl.ds(pl.multiple_of(pl.program_id(0) * tile, tile), tile)
    low_rank = mul(q_ref[...], n_ref[...], TN)
    grad = mul(a_ref[:, at], g_ref[...], TN)
    error_ref[...] = grad + e_ref[at, :] - low_rank
    update_ref[...] = low_rank.astype(BF16)


def run_finish(a, g, e, q, n):
    rows, columns = e.shape
    tile = min(256, rows)

    def whole(x):
        return pl.BlockSpec(x.shape, lambda i: (0, 0))

    def tall(x):
        return pl.BlockSpec((x.shape[0], tile), lambda i: (0, i))

    flat = pl.BlockSpec((tile, columns), lambda i: (i, 0))
    vmem = pl.BlockSpec(memory_space=pltpu.VMEM)
    return pl.pallas_call(
        finish,
        out_shape=(jax.ShapeDtypeStruct(e.shape, F32), jax.ShapeDtypeStruct(e.shape, BF16)),
        grid=(rows // tile,),
        in_specs=[vmem, vmem, vmem, tall(q), whole(n)],
        out_specs=(flat, flat),
        compiler_params=pltpu.CompilerParams(vmem_limit_bytes=VMEM_BYTES),
        name="finish",
    )(*(pltpu.with_memory_space_constraint(x, pltpu.VMEM) for x in (a, g, e)), q, n)


def solution(mesh):
    sizes = (mesh.shape["replica"], mesh.shape["fsdp"], mesh.shape["tensor"])

    def body(attn_out, out_grad, error_in, factor_in):
        q, factor, n, held, activations, cotangents = run_front(
            sizes, attn_out, out_grad, factor_in.T, error_in[0]
        )
        new_error, update = run_finish(activations, cotangents, held, q, n)
        return new_error[None], update, factor.T

    placed = (
        P(("replica", "tensor"), "fsdp"),
        P(("replica", "fsdp"), "tensor"),
        P("replica", "fsdp", "tensor"),
        P("tensor", None),
    )
    return jax.shard_map(
        body,
        mesh=mesh,
        in_specs=placed,
        out_specs=(P("replica", "fsdp", "tensor"), P("fsdp", "tensor"), P("tensor", None)),
        check_vma=False,
    )
```

```python
import functools

import jax
import jax.numpy as jnp
from jax import lax
from jax.experimental import pallas as pl
from jax.experimental.pallas import tpu as pltpu
from jax.sharding import PartitionSpec as P

MESH = pl.DeviceIdType.MESH
HIGHEST = lax.Precision.HIGHEST
F32, BF16 = jnp.float32, jnp.bfloat16
LANE = 128
NN = (((1,), (0,)), ((), ()))
NT = (((1,), (1,)), ((), ()))
TN = (((0,), (0,)), ((), ()))
VMEM_BYTES = 20 * 1024 * 1024
PIECES = 16
PACE = {
    "start": (2, 1, 0),
    "left1": (1, 1, 0),
    "left2": (1, 1, 1),
    "left3": (1, 1, 1),
    "sum": (1, 1, 1),
    "share": (1, 1, 1),
    "spread": (2, 1, 2),
    "right": (5, 4, 2),
    "factor": (2, 3, 4),
    "return": (0, 2, 3),
    "end": (PIECES, PIECES, PIECES),
}


def mul(a, b, dims=NN, precision=None):
    return lax.dot_general(a, b, dims, precision=precision, preferred_element_type=F32)


def split(x):
    high = x.astype(BF16)
    return high, (x - high.astype(F32)).astype(BF16)


def stacked(x):
    return jnp.concatenate(split(x), axis=0)


def folded(x):
    half = x.shape[0] // 2
    return x[:half] + x[half:]


def slabs(rows):
    width = max(LANE, rows // PIECES)
    return width, rows // width


class Cut:
    def __init__(self, rows, columns, pieces):
        self.down = 1
        while (columns * self.down) % (pieces * LANE) != 0:
            self.down *= 2
        self.across = pieces // self.down
        self.rows, self.columns = rows // self.down, columns // self.across

    def at(self, piece, start=0):
        row = pl.multiple_of((piece // self.across) * self.rows, 8)
        column = pl.multiple_of(start + (piece % self.across) * self.columns, LANE)
        return pl.ds(row, self.rows), pl.ds(column, self.columns)


def inverse_factor(gram):
    rank = gram.shape[0]
    row_at = lax.broadcasted_iota(jnp.int32, (rank, LANE), 0)
    lane_at = lax.broadcasted_iota(jnp.int32, (rank, LANE), 1)
    table = gram + jnp.where(lane_at == row_at + LANE // 2, 1.0, 0.0).astype(F32)
    for k in range(rank):
        row = table[k : k + 1, :]
        inverse = 1.0 / jnp.sqrt(row[:, k : k + 1])
        row = row * inverse
        column = jnp.where(row_at > k, table[:, k : k + 1] * inverse, 0.0)
        table = jnp.where(row_at == k, jnp.broadcast_to(row, table.shape), table - column * row)
    return table[:, LANE // 2 : LANE // 2 + rank]


def front(
    sizes,
    a_ref, g_ref, f_ref, e_ref,
    q_out, n_out, nt_out, e_mem, a_all, g_all,
    q_ref, n_ref, nt_ref,
    f_raw, f_mem, part, left, got_rep, mid, got_ten, gf_out, gf_slots, gram_slots, al_out, al_slots,
    n_part, n_got, n_full,
    e_sem, result_sem, own_sem, out_sem, near_sem, ring_sem, g_sem, gf_sem, rep_sem, ten_sem, ten_back, rep_back, gram_sem, al_sem, n_sem, n_back,
):
    reps, fs, ts = sizes
    r, f, t = lax.axis_index("replica"), lax.axis_index("fsdp"), lax.axis_index("tensor")
    rank, rows = part.shape
    block = rows // reps
    tile = min(512, block)
    per = block // tile
    tok_g, tok_a = g_ref.shape[0], a_ref.shape[0]
    width, pieces = slabs(rows)

    def row_copy(step):
        q = lax.rem(r + 1 + step // per, reps)
        at = pl.ds(pl.multiple_of(q * block + (step % per) * tile, tile), tile)
        return pltpu.make_async_copy(e_ref.at[at], e_mem.at[at], e_sem.at[step])

    plane = [(df, dt) for df in range(fs) for dt in range(ts) if df + dt > 0]
    sheet = [(dr, df) for dr in range(reps) for df in range(fs) if dr + df > 0]

    def in_plane(df, dt):
        return {"replica": r, "fsdp": lax.rem(f + df, fs), "tensor": lax.rem(t + dt, ts)}

    def in_sheet(dr, df):
        return {"replica": lax.rem(r + dr, reps), "fsdp": lax.rem(f + df, fs), "tensor": t}

    barrier = pltpu.get_barrier_semaphore()
    greeted = [in_plane(*d) for d in plane] + [in_sheet(*d) for d in sheet if d[0] > 0]
    for device in greeted:
        pl.semaphore_signal(barrier, inc=1, device_id=device, device_id_type=MESH)

    g_own = pl.ds(pl.multiple_of(f * tok_g, tok_g), tok_g)
    a_own = pl.ds(pl.multiple_of(t * tok_a, tok_a), tok_a)
    own_copies = [
        pltpu.make_async_copy(f_ref, f_raw, own_sem.at[0]),
        pltpu.make_async_copy(g_ref, g_all.at[g_own], own_sem.at[1]),
        pltpu.make_async_copy(a_ref, a_all.at[a_own], own_sem.at[2]),
    ]
    for copy in own_copies:
        copy.start()
    own_copies[0].wait()
    high, low = split(f_raw[...])
    wide = jnp.concatenate(
        [high.astype(F32), low.astype(F32), jnp.zeros((LANE - 2 * rank, f_ref.shape[1]), F32)], axis=0
    )
    f_mem[...] = wide.T.astype(BF16)

    me_plane = f * ts + t
    chunk, a_parts, g_parts = gf_out.shape[2], al_out.shape[0], gf_out.shape[0]

    def meets(f_at, t_at):
        return (t_at // g_parts == f_at) if a_parts == 1 else (f_at // a_parts == t_at)

    own_copies[1].wait()
    own_copies[2].wait()
    for step in range(reps * per):
        row_copy(step).start()
    gf = folded(mul(g_all[g_own, :], f_mem[...]).T[: 2 * rank])
    for j in range(g_parts):
        gf_out[j] = gf[:, j * chunk : (j + 1) * chunk]

    @pl.when(meets(f, t))
    def _():
        gf_slots[me_plane] = gf_out[lax.rem(t, g_parts)]

    pl.semaphore_wait(barrier, len(greeted))

    def spread(source, slots, sems, goes, comes):
        copies = []
        for i, (df, dt) in enumerate(plane):
            to_f, to_t = lax.rem(f + df, fs), lax.rem(t + dt, ts)
            from_f, from_t = lax.rem(f + fs - df, fs), lax.rem(t + ts - dt, ts)
            copy = pltpu.make_async_remote_copy(
                src_ref=source(to_f, to_t), dst_ref=slots.at[me_plane],
                send_sem=sems.at[0, i], recv_sem=sems.at[1, i],
                device_id=in_plane(df, dt), device_id_type=MESH,
            )
            sends = goes(to_f, to_t)
            pl.when(sends)(copy.start)
            copies.append((copy, sends, comes(from_f, from_t)))
        return copies

    def settle(copies):
        for copy, sends, receives in copies:
            pl.when(receives)(copy.wait_recv)
            pl.when(sends)(copy.wait_send)

    gf_copies = spread(
        lambda to_f, to_t: gf_out.at[lax.rem(to_t, g_parts)], gf_slots, gf_sem,
        lambda to_f, to_t: meets(f, to_t), lambda from_f, from_t: meets(from_f, t),
    )

    g_copies = []
    for df in range(1, fs):
        copy = pltpu.make_async_remote_copy(
            src_ref=g_all.at[g_own], dst_ref=g_all.at[g_own],
            send_sem=g_sem.at[0, df - 1], recv_sem=g_sem.at[1, df - 1],
            device_id=in_plane(df, 0), device_id_type=MESH,
        )
        copy.start()
        g_copies.append(copy)


    def part_of(block_at, p):
        return (
            pl.ds(pl.multiple_of(lax.rem(block_at + ts, ts) * tok_a, tok_a), tok_a),
            pl.ds(p * width, width),
        )

    def whole_of(block_at):
        return (
            pl.ds(pl.multiple_of(lax.rem(block_at + ts, ts) * tok_a, tok_a), tok_a),
            pl.ds(0, rows),
        )

    def inside(x):
        return jnp.logical_and(x >= 0, x < ts)

    def lands_at(way, d, p):
        return ring_sem.at[way, p] if d == 2 else near_sem.at[way, d - 1]

    def bulk(way, d, p):
        sign = 1 - 2 * way
        block_at = t if d <= 2 else t - sign * (d - 1)
        dest = t + sign * (d if d <= 2 else 1)
        at = part_of(block_at, p)
        copy = pltpu.make_async_remote_copy(
            src_ref=a_all.at[at], dst_ref=a_all.at[at],
            send_sem=out_sem.at[way, d - 1], recv_sem=lands_at(way, d, p),
            device_id={"replica": r, "fsdp": f, "tensor": lax.rem(dest + ts, ts)},
            device_id_type=MESH,
        )
        return copy, jnp.logical_and(inside(block_at), inside(dest))

    def send(d, p):
        if d >= ts:
            return
        for way in range(2):
            copy, valid = bulk(way, d, p)
            pl.when(valid)(copy.start)

    def came(way, d, at, sem):
        copy = pltpu.make_async_remote_copy(
            src_ref=a_all.at[at], dst_ref=a_all.at[at], send_sem=out_sem.at[way, d - 1], recv_sem=sem,
            device_id=in_plane(0, 1), device_id_type=MESH,
        )
        pl.when(inside(t - (1 - 2 * way) * d))(copy.wait_recv)

    landed = set()

    def land(d, p):
        if (d, p) in landed:
            return
        landed.add((d, p))
        for way in range(2):
            came(way, d, part_of(t - (1 - 2 * way) * d, p), lands_at(way, d, p))

    def land_whole(d):
        if d == 2:
            for p in range(pieces):
                land(2, p)
        elif (d, -1) not in landed:
            landed.add((d, -1))
            for way in range(2):
                came(way, d, whole_of(t - (1 - 2 * way) * d), near_sem.at[way, d - 1])

    sent = [0, 0, 0]

    def inject(phase):
        far, near, onward = PACE.get(phase, (0, 0, 0))
        for _ in range(min(far, pieces - sent[0])):
            send(2, sent[0])
            sent[0] += 1
        for _ in range(min(onward, sent[0] - sent[2]) if ts > 3 else 0):
            land(2, sent[2])
            send(3, sent[2])
            sent[2] += 1
        for _ in range(min(near, pieces - sent[1])):
            send(1, sent[1])
            sent[1] += 1

    inject("start")

    rep_copies = []
    for dr in range(1, reps + 1):
        q = lax.rem(r + dr, reps)
        base = pl.multiple_of(q * block, LANE)
        inject(f"left{dr}")

        def tile_left(j, _, dr=dr, base=base):
            row_copy((dr - 1) * per + j).wait()
            at = pl.ds(pl.multiple_of(base + j * tile, tile), tile)
            eh, el = split(e_mem[at, :])
            total = mul(jnp.concatenate([eh, el], axis=0), f_mem[...])
            total = total[:tile] + total[tile:]
            part[:, at] = folded(total.T[: 2 * rank])
            return 0

        lax.fori_loop(0, per, tile_left, 0)
        if dr == 1:
            settle(gf_copies)
            first = (t * tok_a) // tok_g
            totals = []
            for j in range(a_parts):
                total = gf_slots[(first + j) * ts]
                for dt in range(1, ts):
                    total = total + gf_slots[(first + j) * ts + dt]
                totals.append(total)
            own = stacked(jnp.concatenate(totals, axis=1))
        at = pl.ds(base, block)
        part[:, at] += folded(mul(own, a_all[a_own, at]))
        if dr < reps:
            copy = pltpu.make_async_remote_copy(
                src_ref=part.at[:, at], dst_ref=got_rep.at[dr - 1],
                send_sem=rep_sem.at[0, dr - 1], recv_sem=rep_sem.at[1, dr - 1],
                device_id=in_sheet(dr, 0), device_id_type=MESH,
            )
            copy.start()
            rep_copies.append(copy)

    mine = pl.ds(pl.multiple_of(r * block, LANE), block)
    total = part[:, mine]
    for i, copy in enumerate(rep_copies):
        copy.wait()
        total = total + got_rep[i]
    mid[...] = total

    cut = Cut(rank, block, ts)
    ten_copies = []
    for dt in range(1, ts):
        copy = pltpu.make_async_remote_copy(
            src_ref=mid.at[cut.at(lax.rem(t + dt, ts))], dst_ref=got_ten.at[dt - 1],
            send_sem=ten_sem.at[0, dt - 1], recv_sem=ten_sem.at[1, dt - 1],
            device_id=in_plane(0, dt), device_id_type=MESH,
        )
        copy.start()
        ten_copies.append(copy)
    inject("sum")
    total = mid[cut.at(t)]
    for i, copy in enumerate(ten_copies):
        copy.wait()
        total = total + got_ten[i]
    own = cut.at(t, r * block)
    left[own] = total * (1.0 / reps)
    back = []
    for dt in range(1, ts):
        copy = pltpu.make_async_remote_copy(
            src_ref=left.at[own], dst_ref=left.at[own],
            send_sem=ten_back.at[0, dt - 1], recv_sem=ten_back.at[1, dt - 1],
            device_id=in_plane(0, dt), device_id_type=MESH,
        )
        copy.start()
        back.append(copy)
    inject("share")
    for copy in back:
        copy.wait()
    back = []
    for dr in range(1, reps):
        copy = pltpu.make_async_remote_copy(
            src_ref=left.at[:, mine], dst_ref=left.at[:, mine],
            send_sem=rep_back.at[0, dr - 1], recv_sem=rep_back.at[1, dr - 1],
            device_id=in_sheet(dr, 0), device_id_type=MESH,
        )
        copy.start()
        back.append(copy)
    inject("spread")
    for copy in back:
        copy.wait()

    whole = left[...]
    al = folded(mul(stacked(whole), a_all[a_own, :], NT))
    for j in range(a_parts):
        al_out[j] = al[:, j * chunk : (j + 1) * chunk]

    @pl.when(meets(f, t))
    def _():
        al_slots[me_plane] = al_out[lax.rem(f, a_parts)]

    al_copies = spread(
        lambda to_f, to_t: al_out.at[lax.rem(to_f, a_parts)], al_slots, al_sem,
        lambda to_f, to_t: meets(to_f, t), lambda from_f, from_t: meets(f, from_t),
    )
    inject("right")
    gram_slots[f, :, 0:rank] = mul(whole, whole, NT, HIGHEST)
    gram_slots[f, :, rank:LANE] = jnp.zeros((rank, LANE - rank), F32)
    gram_copies = []
    for df in range(1, fs):
        copy = pltpu.make_async_remote_copy(
            src_ref=gram_slots.at[f], dst_ref=gram_slots.at[f],
            send_sem=gram_sem.at[0, df - 1], recv_sem=gram_sem.at[1, df - 1],
            device_id=in_plane(df, 0), device_id_type=MESH,
        )
        copy.start()
        gram_copies.append(copy)

    n_part[...] = jnp.zeros(n_part.shape, F32)

    def tile_right(j, _):
        at = pl.ds(pl.multiple_of(j * tile, tile), tile)
        eh, el = split(e_mem[at, :])
        both = stacked(left[:, at])
        n_part[...] += folded(mul(jnp.concatenate([both, both], axis=1), jnp.concatenate([eh, el], axis=0)))
        return 0

    lax.fori_loop(0, rows // tile, tile_right, 0)

    settle(al_copies)
    first = (f * tok_g) // tok_a
    totals = []
    for j in range(g_parts):
        total = al_slots[first + j]
        for df in range(1, fs):
            total = total + al_slots[df * ts + first + j]
        totals.append(total)
    tokens = stacked(jnp.concatenate(totals, axis=1))
    n_part[...] += folded(mul(tokens, g_all[g_own, :]))

    n_cut = Cut(rank, n_part.shape[1], reps * fs)
    n_copies = []
    for i, (dr, df) in enumerate(sheet):
        owner = lax.rem(r + dr, reps) * fs + lax.rem(f + df, fs)
        copy = pltpu.make_async_remote_copy(
            src_ref=n_part.at[n_cut.at(owner)], dst_ref=n_got.at[i],
            send_sem=n_sem.at[0, i], recv_sem=n_sem.at[1, i],
            device_id=in_sheet(dr, df), device_id_type=MESH,
        )
        copy.start()
        n_copies.append(copy)

    inject("factor")
    for copy in gram_copies:
        copy.wait()
    gram = gram_slots[0]
    for df in range(1, fs):
        gram = gram + gram_slots[df]
    inverse = inverse_factor(gram)
    high, low = split(mul(inverse, left[...], precision=HIGHEST))
    q_ref[0:rank] = high
    q_ref[rank : 2 * rank] = low
    q_ref[2 * rank :] = high

    place = n_cut.at(r * fs + f)
    total = n_part[place]
    for i, copy in enumerate(n_copies):
        copy.wait()
        total = total + n_got[i]
    n_full[place] = total * (1.0 / reps)
    back = []
    for i, (dr, df) in enumerate(sheet):
        copy = pltpu.make_async_remote_copy(
            src_ref=n_full.at[place], dst_ref=n_full.at[place],
            send_sem=n_back.at[0, i], recv_sem=n_back.at[1, i],
            device_id=in_sheet(dr, df), device_id_type=MESH,
        )
        copy.start()
        back.append(copy)
    inject("return")
    for copy in back:
        copy.wait()
    factor = mul(inverse, n_full[...], precision=HIGHEST)
    n_ref[...] = factor
    high, low = split(factor)
    nt_ref[0:rank] = high
    nt_ref[rank : 2 * rank] = high
    nt_ref[2 * rank :] = low

    out_copies = [
        pltpu.make_async_copy(source, target, result_sem.at[i])
        for i, (source, target) in enumerate(((q_ref, q_out), (n_ref, n_out), (nt_ref, nt_out)))
    ]
    for copy in out_copies:
        copy.start()
    inject("end")
    for copy in out_copies:
        copy.wait()
    for copy in g_copies:
        copy.wait()
    for d in range(4, ts):
        land_whole(d - 1)
        for p in range(pieces):
            send(d, p)
    for d in range(1, ts):
        land_whole(d)
        for way in range(2):
            sign = 1 - 2 * way
            source = t if d <= 2 else t - sign * (d - 1)
            target = t + sign * (d if d <= 2 else 1)
            at = whole_of(t - sign * d)
            copy = pltpu.make_async_remote_copy(
                src_ref=a_all.at[at], dst_ref=a_all.at[at],
                send_sem=out_sem.at[way, d - 1], recv_sem=near_sem.at[way, d - 1],
                device_id=in_plane(0, 1), device_id_type=MESH,
            )
            pl.when(jnp.logical_and(inside(source), inside(target)))(copy.wait_send)


def run_front(sizes, a, g, f, e):
    reps, fs, ts = sizes
    rank, rows, columns = f.shape[0], e.shape[0], e.shape[1]
    tok_g, tok_a = g.shape[0], a.shape[0]
    block, chunk = rows // reps, min(tok_a, tok_g)
    cut, n_cut = Cut(rank, block, ts), Cut(rank, columns, reps * fs)
    tiles = rows // min(512, block)
    plane, sheet = fs * ts - 1, reps * fs - 1
    vmem = pl.BlockSpec(memory_space=pltpu.VMEM)
    dma = pltpu.SemaphoreType.DMA
    return pl.pallas_call(
        functools.partial(front, sizes),
        out_shape=(
            jax.ShapeDtypeStruct((3 * rank, rows), BF16),
            jax.ShapeDtypeStruct((rank, columns), F32),
            jax.ShapeDtypeStruct((3 * rank, columns), BF16),
            pltpu.VMEM((rows, columns), F32),
            pltpu.VMEM((tok_a * ts, rows), BF16),
            pltpu.VMEM((tok_g * fs, columns), BF16),
        ),
        in_specs=[pl.BlockSpec(memory_space=pl.ANY)] * 4,
        out_specs=(pl.BlockSpec(memory_space=pl.ANY),) * 3 + (vmem,) * 3,
        scratch_shapes=[
            pltpu.VMEM((3 * rank, rows), BF16),
            pltpu.VMEM((rank, columns), F32),
            pltpu.VMEM((3 * rank, columns), BF16),
            pltpu.VMEM((rank, columns), F32),
            pltpu.VMEM((columns, LANE), BF16),
            pltpu.VMEM((rank, rows), F32),
            pltpu.VMEM((rank, rows), F32),
            pltpu.VMEM((reps - 1, rank, block), F32),
            pltpu.VMEM((rank, block), F32),
            pltpu.VMEM((ts - 1, cut.rows, cut.columns), F32),
            pltpu.VMEM((tok_g // chunk, rank, chunk), F32),
            pltpu.VMEM((fs * ts, rank, chunk), F32),
            pltpu.VMEM((fs, rank, LANE), F32),
            pltpu.VMEM((tok_a // chunk, rank, chunk), F32),
            pltpu.VMEM((fs * ts, rank, chunk), F32),
            pltpu.VMEM((rank, columns), F32),
            pltpu.VMEM((sheet, n_cut.rows, n_cut.columns), F32),
            pltpu.VMEM((rank, columns), F32),
            dma((tiles,)), dma((3,)), dma((3,)), dma((2, ts)), dma((2, ts)), dma((2, PIECES)), dma((2, fs)), dma((2, plane)), dma((2, reps - 1)), dma((2, ts - 1)), dma((2, ts - 1)),
            dma((2, reps - 1)), dma((2, fs)), dma((2, plane)), dma((2, sheet)), dma((2, sheet)),
        ],
        compiler_params=pltpu.CompilerParams(
            collective_id=0, has_side_effects=True, vmem_limit_bytes=VMEM_BYTES
        ),
        cost_estimate=pl.CostEstimate(
            flops=100_000_000_000, bytes_accessed=rows * columns * 8, transcendentals=0
        ),
        name="front",
    )(a, g, f, e)


def finish(a_ref, g_ref, e_ref, q_ref, n_ref, factor_ref, error_ref, update_ref, factor_out):
    tile = error_ref.shape[0]
    at = pl.ds(pl.multiple_of(pl.program_id(0) * tile, tile), tile)
    low_rank = mul(q_ref[...], n_ref[...], TN)
    error_ref[...] = mul(a_ref[:, at], g_ref[...], TN) + e_ref[at, :] - low_rank
    update_ref[...] = low_rank.astype(BF16)
    factor_out[...] = factor_ref[...]


def run_finish(a, g, e, q, n, factor):
    rows, columns = e.shape
    tile = min(512, rows)

    def whole(x):
        return pl.BlockSpec(x.shape, lambda i: (0, 0))

    flat = pl.BlockSpec((tile, columns), lambda i: (i, 0))
    vmem = pl.BlockSpec(memory_space=pltpu.VMEM)
    held = (pltpu.with_memory_space_constraint(x, pltpu.VMEM) for x in (a, g, e))
    return pl.pallas_call(
        finish,
        out_shape=(
            jax.ShapeDtypeStruct(e.shape, F32), jax.ShapeDtypeStruct(e.shape, BF16), jax.ShapeDtypeStruct(factor.shape, F32),
        ),
        grid=(rows // tile,),
        in_specs=[vmem, vmem, vmem, pl.BlockSpec((q.shape[0], tile), lambda i: (0, i)), whole(n), whole(factor)],
        out_specs=(flat, flat, whole(factor)),
        compiler_params=pltpu.CompilerParams(vmem_limit_bytes=VMEM_BYTES),
        name="finish",
    )(*held, q, n, factor)


def solution(mesh):
    sizes = (mesh.shape["replica"], mesh.shape["fsdp"], mesh.shape["tensor"])

    def body(attn_out, out_grad, error_in, factor_in):
        q, factor, n, held, activations, cotangents = run_front(
            sizes, attn_out, out_grad, factor_in.T, error_in[0]
        )
        new_error, update, factor = run_finish(activations, cotangents, held, q, n, factor)
        return new_error[None], update, factor.T

    placed = (
        P(("replica", "tensor"), "fsdp"),
        P(("replica", "fsdp"), "tensor"),
        P("replica", "fsdp", "tensor"),
        P("tensor", None),
    )
    return jax.shard_map(
        body,
        mesh=mesh,
        in_specs=placed,
        out_specs=(P("replica", "fsdp", "tensor"), P("fsdp", "tensor"), P("tensor", None)),
        check_vma=False,
    )
```

```python
import functools

import jax
import jax.numpy as jnp
from jax import lax
from jax.experimental import pallas as pl
from jax.experimental.pallas import tpu as pltpu
from jax.sharding import PartitionSpec as P

MESH = pl.DeviceIdType.MESH
HIGHEST = lax.Precision.HIGHEST
F32, BF16 = jnp.float32, jnp.bfloat16
LANE = 128
NN = (((1,), (0,)), ((), ()))
NT = (((1,), (1,)), ((), ()))
TN = (((0,), (0,)), ((), ()))
VMEM_BYTES = 20 * 1024 * 1024
PIECES = 16
PACE = {
    "start": (2, 1, 0),
    "left1": (2, 0, 0),
    "left2": (1, 1, 1),
    "left3": (1, 1, 2),
    "sum": (1, 1, 1),
    "share": (1, 1, 1),
    "spread": (2, 1, 2),
    "right": (5, 4, 2),
    "factor": (1, 4, 4),
    "return": (0, 2, 3),
    "end": (PIECES, PIECES, PIECES),
}


def mul(a, b, dims=NN, precision=None):
    return lax.dot_general(a, b, dims, precision=precision, preferred_element_type=F32)


def split(x):
    high = x.astype(BF16)
    return high, (x - high.astype(F32)).astype(BF16)


def stacked(x):
    return jnp.concatenate(split(x), axis=0)


def folded(x):
    half = x.shape[0] // 2
    return x[:half] + x[half:]


def slabs(rows):
    width = max(LANE, rows // PIECES)
    return width, rows // width


class Cut:
    def __init__(self, rows, columns, pieces):
        self.down = 1
        while (columns * self.down) % (pieces * LANE) != 0:
            self.down *= 2
        self.across = pieces // self.down
        self.rows, self.columns = rows // self.down, columns // self.across

    def at(self, piece, start=0):
        row = pl.multiple_of((piece // self.across) * self.rows, 8)
        column = pl.multiple_of(start + (piece % self.across) * self.columns, LANE)
        return pl.ds(row, self.rows), pl.ds(column, self.columns)


def inverse_factor(gram):
    rank = gram.shape[0]
    row_at = lax.broadcasted_iota(jnp.int32, (rank, LANE), 0)
    lane_at = lax.broadcasted_iota(jnp.int32, (rank, LANE), 1)
    table = gram + jnp.where(lane_at == row_at + LANE // 2, 1.0, 0.0).astype(F32)
    for k in range(rank):
        row = table[k : k + 1, :]
        inverse = 1.0 / jnp.sqrt(row[:, k : k + 1])
        row = row * inverse
        column = jnp.where(row_at > k, table[:, k : k + 1] * inverse, 0.0)
        table = jnp.where(row_at == k, jnp.broadcast_to(row, table.shape), table - column * row)
    return table[:, LANE // 2 : LANE // 2 + rank]


def front(
    sizes,
    a_ref, g_ref, f_ref, e_ref,
    q_out, n_out, nt_out, e_mem, a_all, g_all,
    q_ref, n_ref, nt_ref,
    f_raw, f_mem, part, left, got_rep, mid, got_ten, gf_out, gf_slots, gram_slots, al_out, al_slots,
    n_part, n_got, n_full,
    e_sem, result_sem, own_sem, out_sem, near_sem, ring_sem, g_sem, gf_sem, rep_sem, ten_sem, ten_back, rep_back, gram_sem, al_sem, n_sem, n_back,
):
    reps, fs, ts = sizes
    r, f, t = lax.axis_index("replica"), lax.axis_index("fsdp"), lax.axis_index("tensor")
    rank, rows = part.shape
    block = rows // reps
    tile = min(512, block)
    per = block // tile
    tok_g, tok_a = g_ref.shape[0], a_ref.shape[0]
    width, pieces = slabs(rows)

    def row_copy(step):
        q = lax.rem(r + 1 + step // per, reps)
        at = pl.ds(pl.multiple_of(q * block + (step % per) * tile, tile), tile)
        return pltpu.make_async_copy(e_ref.at[at], e_mem.at[at], e_sem.at[step])

    plane = [(df, dt) for df in range(fs) for dt in range(ts) if df + dt > 0]
    sheet = [(dr, df) for dr in range(reps) for df in range(fs) if dr + df > 0]

    def in_plane(df, dt):
        return {"replica": r, "fsdp": lax.rem(f + df, fs), "tensor": lax.rem(t + dt, ts)}

    def in_sheet(dr, df):
        return {"replica": lax.rem(r + dr, reps), "fsdp": lax.rem(f + df, fs), "tensor": t}

    barrier = pltpu.get_barrier_semaphore()
    greeted = [in_plane(*d) for d in plane] + [in_sheet(*d) for d in sheet if d[0] > 0]
    for device in greeted:
        pl.semaphore_signal(barrier, inc=1, device_id=device, device_id_type=MESH)

    g_own = pl.ds(pl.multiple_of(f * tok_g, tok_g), tok_g)
    a_own = pl.ds(pl.multiple_of(t * tok_a, tok_a), tok_a)
    own_copies = [
        pltpu.make_async_copy(f_ref, f_raw, own_sem.at[0]),
        pltpu.make_async_copy(g_ref, g_all.at[g_own], own_sem.at[1]),
        pltpu.make_async_copy(a_ref, a_all.at[a_own], own_sem.at[2]),
    ]
    for copy in own_copies:
        copy.start()
    own_copies[0].wait()
    high, low = split(f_raw[...])
    wide = jnp.concatenate(
        [high.astype(F32), low.astype(F32), jnp.zeros((LANE - 2 * rank, f_ref.shape[1]), F32)], axis=0
    )
    f_mem[...] = wide.T.astype(BF16)

    me_plane = f * ts + t
    chunk, a_parts, g_parts = gf_out.shape[2], al_out.shape[0], gf_out.shape[0]

    def meets(f_at, t_at):
        return (t_at // g_parts == f_at) if a_parts == 1 else (f_at // a_parts == t_at)

    own_copies[1].wait()
    own_copies[2].wait()
    for step in range(reps * per):
        row_copy(step).start()
    gf = folded(mul(g_all[g_own, :], f_mem[...]).T[: 2 * rank])
    for j in range(g_parts):
        gf_out[j] = gf[:, j * chunk : (j + 1) * chunk]

    @pl.when(meets(f, t))
    def _():
        gf_slots[me_plane] = gf_out[lax.rem(t, g_parts)]

    pl.semaphore_wait(barrier, len(greeted))

    def spread(source, slots, sems, goes, comes):
        copies = []
        for i, (df, dt) in enumerate(plane):
            to_f, to_t = lax.rem(f + df, fs), lax.rem(t + dt, ts)
            from_f, from_t = lax.rem(f + fs - df, fs), lax.rem(t + ts - dt, ts)
            copy = pltpu.make_async_remote_copy(
                src_ref=source(to_f, to_t), dst_ref=slots.at[me_plane],
                send_sem=sems.at[0, i], recv_sem=sems.at[1, i],
                device_id=in_plane(df, dt), device_id_type=MESH,
            )
            sends = goes(to_f, to_t)
            pl.when(sends)(copy.start)
            copies.append((copy, sends, comes(from_f, from_t)))
        return copies

    def settle(copies):
        for copy, sends, receives in copies:
            pl.when(receives)(copy.wait_recv)
            pl.when(sends)(copy.wait_send)

    gf_copies = spread(
        lambda to_f, to_t: gf_out.at[lax.rem(to_t, g_parts)], gf_slots, gf_sem,
        lambda to_f, to_t: meets(f, to_t), lambda from_f, from_t: meets(from_f, t),
    )

    g_copies = []
    for df in range(1, fs):
        copy = pltpu.make_async_remote_copy(
            src_ref=g_all.at[g_own], dst_ref=g_all.at[g_own],
            send_sem=g_sem.at[0, df - 1], recv_sem=g_sem.at[1, df - 1],
            device_id=in_plane(df, 0), device_id_type=MESH,
        )
        copy.start()
        g_copies.append(copy)


    def part_of(block_at, p):
        return (
            pl.ds(pl.multiple_of(lax.rem(block_at + ts, ts) * tok_a, tok_a), tok_a),
            pl.ds(p * width, width),
        )

    def whole_of(block_at):
        return (
            pl.ds(pl.multiple_of(lax.rem(block_at + ts, ts) * tok_a, tok_a), tok_a),
            pl.ds(0, rows),
        )

    def inside(x):
        return jnp.logical_and(x >= 0, x < ts)

    def lands_at(way, d, p):
        return ring_sem.at[way, p] if d == 2 else near_sem.at[way, d - 1]

    def bulk(way, d, p):
        sign = 1 - 2 * way
        block_at = t if d <= 2 else t - sign * (d - 1)
        dest = t + sign * (d if d <= 2 else 1)
        at = part_of(block_at, p)
        copy = pltpu.make_async_remote_copy(
            src_ref=a_all.at[at], dst_ref=a_all.at[at],
            send_sem=out_sem.at[way, d - 1], recv_sem=lands_at(way, d, p),
            device_id={"replica": r, "fsdp": f, "tensor": lax.rem(dest + ts, ts)},
            device_id_type=MESH,
        )
        return copy, jnp.logical_and(inside(block_at), inside(dest))

    def send(d, p):
        if d >= ts:
            return
        for way in range(2):
            copy, valid = bulk(way, d, p)
            pl.when(valid)(copy.start)

    def came(way, d, at, sem):
        copy = pltpu.make_async_remote_copy(
            src_ref=a_all.at[at], dst_ref=a_all.at[at], send_sem=out_sem.at[way, d - 1], recv_sem=sem,
            device_id=in_plane(0, 1), device_id_type=MESH,
        )
        pl.when(inside(t - (1 - 2 * way) * d))(copy.wait_recv)

    landed = set()

    def land(d, p):
        if (d, p) in landed:
            return
        landed.add((d, p))
        for way in range(2):
            came(way, d, part_of(t - (1 - 2 * way) * d, p), lands_at(way, d, p))

    def land_whole(d):
        if d == 2:
            for p in range(pieces):
                land(2, p)
        elif (d, -1) not in landed:
            landed.add((d, -1))
            for way in range(2):
                came(way, d, whole_of(t - (1 - 2 * way) * d), near_sem.at[way, d - 1])

    sent = [0, 0, 0]

    def inject(phase):
        far, near, onward = PACE.get(phase, (0, 0, 0))
        for _ in range(min(far, pieces - sent[0])):
            send(2, sent[0])
            sent[0] += 1
        for _ in range(min(onward, sent[0] - sent[2]) if ts > 3 else 0):
            land(2, sent[2])
            send(3, sent[2])
            sent[2] += 1
        for _ in range(min(near, pieces - sent[1])):
            send(1, sent[1])
            sent[1] += 1

    inject("start")

    rep_copies = []
    for dr in range(1, reps + 1):
        q = lax.rem(r + dr, reps)
        base = pl.multiple_of(q * block, LANE)
        inject(f"left{dr}")

        def tile_left(j, _, dr=dr, base=base):
            row_copy((dr - 1) * per + j).wait()
            at = pl.ds(pl.multiple_of(base + j * tile, tile), tile)
            eh, el = split(e_mem[at, :])
            total = mul(jnp.concatenate([eh, el], axis=0), f_mem[...])
            total = total[:tile] + total[tile:]
            part[:, at] = folded(total.T[: 2 * rank])
            return 0

        lax.fori_loop(0, per, tile_left, 0)
        if dr == 1:
            settle(gf_copies)
            first = (t * tok_a) // tok_g
            totals = []
            for j in range(a_parts):
                total = gf_slots[(first + j) * ts]
                for dt in range(1, ts):
                    total = total + gf_slots[(first + j) * ts + dt]
                totals.append(total)
            own = stacked(jnp.concatenate(totals, axis=1))
        at = pl.ds(base, block)
        part[:, at] += folded(mul(own, a_all[a_own, at]))
        if dr < reps:
            copy = pltpu.make_async_remote_copy(
                src_ref=part.at[:, at], dst_ref=got_rep.at[dr - 1],
                send_sem=rep_sem.at[0, dr - 1], recv_sem=rep_sem.at[1, dr - 1],
                device_id=in_sheet(dr, 0), device_id_type=MESH,
            )
            copy.start()
            rep_copies.append(copy)

    mine = pl.ds(pl.multiple_of(r * block, LANE), block)
    total = part[:, mine]
    for i, copy in enumerate(rep_copies):
        copy.wait()
        total = total + got_rep[i]
    mid[...] = total

    cut = Cut(rank, block, ts)
    ten_copies = []
    for dt in range(1, ts):
        copy = pltpu.make_async_remote_copy(
            src_ref=mid.at[cut.at(lax.rem(t + dt, ts))], dst_ref=got_ten.at[dt - 1],
            send_sem=ten_sem.at[0, dt - 1], recv_sem=ten_sem.at[1, dt - 1],
            device_id=in_plane(0, dt), device_id_type=MESH,
        )
        copy.start()
        ten_copies.append(copy)
    inject("sum")
    total = mid[cut.at(t)]
    for i, copy in enumerate(ten_copies):
        copy.wait()
        total = total + got_ten[i]
    own = cut.at(t, r * block)
    left[own] = total * (1.0 / reps)
    back = []
    for dt in range(1, ts):
        copy = pltpu.make_async_remote_copy(
            src_ref=left.at[own], dst_ref=left.at[own],
            send_sem=ten_back.at[0, dt - 1], recv_sem=ten_back.at[1, dt - 1],
            device_id=in_plane(0, dt), device_id_type=MESH,
        )
        copy.start()
        back.append(copy)
    inject("share")
    for copy in back:
        copy.wait()
    back = []
    for dr in range(1, reps):
        copy = pltpu.make_async_remote_copy(
            src_ref=left.at[:, mine], dst_ref=left.at[:, mine],
            send_sem=rep_back.at[0, dr - 1], recv_sem=rep_back.at[1, dr - 1],
            device_id=in_sheet(dr, 0), device_id_type=MESH,
        )
        copy.start()
        back.append(copy)
    inject("spread")
    for copy in back:
        copy.wait()

    whole = left[...]
    al = folded(mul(stacked(whole), a_all[a_own, :], NT))
    for j in range(a_parts):
        al_out[j] = al[:, j * chunk : (j + 1) * chunk]

    @pl.when(meets(f, t))
    def _():
        al_slots[me_plane] = al_out[lax.rem(f, a_parts)]

    al_copies = spread(
        lambda to_f, to_t: al_out.at[lax.rem(to_f, a_parts)], al_slots, al_sem,
        lambda to_f, to_t: meets(to_f, t), lambda from_f, from_t: meets(f, from_t),
    )
    inject("right")
    gram_slots[f, :, 0:rank] = mul(whole, whole, NT, HIGHEST)
    gram_slots[f, :, rank:LANE] = jnp.zeros((rank, LANE - rank), F32)
    gram_copies = []
    for df in range(1, fs):
        copy = pltpu.make_async_remote_copy(
            src_ref=gram_slots.at[f], dst_ref=gram_slots.at[f],
            send_sem=gram_sem.at[0, df - 1], recv_sem=gram_sem.at[1, df - 1],
            device_id=in_plane(df, 0), device_id_type=MESH,
        )
        copy.start()
        gram_copies.append(copy)

    n_part[...] = jnp.zeros(n_part.shape, F32)

    def tile_right(j, _):
        at = pl.ds(pl.multiple_of(j * tile, tile), tile)
        eh, el = split(e_mem[at, :])
        both = stacked(left[:, at])
        n_part[...] += folded(mul(jnp.concatenate([both, both], axis=1), jnp.concatenate([eh, el], axis=0)))
        return 0

    lax.fori_loop(0, rows // tile, tile_right, 0)

    settle(al_copies)
    first = (f * tok_g) // tok_a
    totals = []
    for j in range(g_parts):
        total = al_slots[first + j]
        for df in range(1, fs):
            total = total + al_slots[df * ts + first + j]
        totals.append(total)
    tokens = stacked(jnp.concatenate(totals, axis=1))
    n_part[...] += folded(mul(tokens, g_all[g_own, :]))

    n_cut = Cut(rank, n_part.shape[1], reps * fs)
    n_copies = []
    for i, (dr, df) in enumerate(sheet):
        owner = lax.rem(r + dr, reps) * fs + lax.rem(f + df, fs)
        copy = pltpu.make_async_remote_copy(
            src_ref=n_part.at[n_cut.at(owner)], dst_ref=n_got.at[i],
            send_sem=n_sem.at[0, i], recv_sem=n_sem.at[1, i],
            device_id=in_sheet(dr, df), device_id_type=MESH,
        )
        copy.start()
        n_copies.append(copy)

    inject("factor")
    for copy in gram_copies:
        copy.wait()
    gram = gram_slots[0]
    for df in range(1, fs):
        gram = gram + gram_slots[df]
    inverse = inverse_factor(gram)
    high, low = split(mul(inverse, left[...], precision=HIGHEST))
    q_ref[0:rank] = high
    q_ref[rank : 2 * rank] = low
    q_ref[2 * rank :] = high

    place = n_cut.at(r * fs + f)
    total = n_part[place]
    for i, copy in enumerate(n_copies):
        copy.wait()
        total = total + n_got[i]
    n_full[place] = total * (1.0 / reps)
    back = []
    for i, (dr, df) in enumerate(sheet):
        copy = pltpu.make_async_remote_copy(
            src_ref=n_full.at[place], dst_ref=n_full.at[place],
            send_sem=n_back.at[0, i], recv_sem=n_back.at[1, i],
            device_id=in_sheet(dr, df), device_id_type=MESH,
        )
        copy.start()
        back.append(copy)
    inject("return")
    for copy in back:
        copy.wait()
    factor = mul(inverse, n_full[...], precision=HIGHEST)
    n_ref[...] = factor
    high, low = split(factor)
    nt_ref[0:rank] = high
    nt_ref[rank : 2 * rank] = high
    nt_ref[2 * rank :] = low

    out_copies = [
        pltpu.make_async_copy(source, target, result_sem.at[i])
        for i, (source, target) in enumerate(((q_ref, q_out), (n_ref, n_out), (nt_ref, nt_out)))
    ]
    for copy in out_copies:
        copy.start()
    inject("end")
    for copy in out_copies:
        copy.wait()
    for copy in g_copies:
        copy.wait()
    for d in range(4, ts):
        land_whole(d - 1)
        for p in range(pieces):
            send(d, p)
    for d in range(1, ts):
        land_whole(d)
        for way in range(2):
            sign = 1 - 2 * way
            source = t if d <= 2 else t - sign * (d - 1)
            target = t + sign * (d if d <= 2 else 1)
            at = whole_of(t - sign * d)
            copy = pltpu.make_async_remote_copy(
                src_ref=a_all.at[at], dst_ref=a_all.at[at],
                send_sem=out_sem.at[way, d - 1], recv_sem=near_sem.at[way, d - 1],
                device_id=in_plane(0, 1), device_id_type=MESH,
            )
            pl.when(jnp.logical_and(inside(source), inside(target)))(copy.wait_send)


def run_front(sizes, a, g, f, e):
    reps, fs, ts = sizes
    rank, rows, columns = f.shape[0], e.shape[0], e.shape[1]
    tok_g, tok_a = g.shape[0], a.shape[0]
    block, chunk = rows // reps, min(tok_a, tok_g)
    cut, n_cut = Cut(rank, block, ts), Cut(rank, columns, reps * fs)
    tiles = rows // min(512, block)
    plane, sheet = fs * ts - 1, reps * fs - 1
    vmem = pl.BlockSpec(memory_space=pltpu.VMEM)
    dma = pltpu.SemaphoreType.DMA
    return pl.pallas_call(
        functools.partial(front, sizes),
        out_shape=(
            jax.ShapeDtypeStruct((3 * rank, rows), BF16),
            jax.ShapeDtypeStruct((rank, columns), F32),
            jax.ShapeDtypeStruct((3 * rank, columns), BF16),
            pltpu.VMEM((rows, columns), F32),
            pltpu.VMEM((tok_a * ts, rows), BF16),
            pltpu.VMEM((tok_g * fs, columns), BF16),
        ),
        in_specs=[pl.BlockSpec(memory_space=pl.ANY)] * 4,
        out_specs=(pl.BlockSpec(memory_space=pl.ANY),) * 3 + (vmem,) * 3,
        scratch_shapes=[
            pltpu.VMEM((3 * rank, rows), BF16),
            pltpu.VMEM((rank, columns), F32),
            pltpu.VMEM((3 * rank, columns), BF16),
            pltpu.VMEM((rank, columns), F32),
            pltpu.VMEM((columns, LANE), BF16),
            pltpu.VMEM((rank, rows), F32),
            pltpu.VMEM((rank, rows), F32),
            pltpu.VMEM((reps - 1, rank, block), F32),
            pltpu.VMEM((rank, block), F32),
            pltpu.VMEM((ts - 1, cut.rows, cut.columns), F32),
            pltpu.VMEM((tok_g // chunk, rank, chunk), F32),
            pltpu.VMEM((fs * ts, rank, chunk), F32),
            pltpu.VMEM((fs, rank, LANE), F32),
            pltpu.VMEM((tok_a // chunk, rank, chunk), F32),
            pltpu.VMEM((fs * ts, rank, chunk), F32),
            pltpu.VMEM((rank, columns), F32),
            pltpu.VMEM((sheet, n_cut.rows, n_cut.columns), F32),
            pltpu.VMEM((rank, columns), F32),
            dma((tiles,)), dma((3,)), dma((3,)), dma((2, ts)), dma((2, ts)), dma((2, PIECES)), dma((2, fs)), dma((2, plane)), dma((2, reps - 1)), dma((2, ts - 1)), dma((2, ts - 1)),
            dma((2, reps - 1)), dma((2, fs)), dma((2, plane)), dma((2, sheet)), dma((2, sheet)),
        ],
        compiler_params=pltpu.CompilerParams(
            collective_id=0, has_side_effects=True, vmem_limit_bytes=VMEM_BYTES
        ),
        cost_estimate=pl.CostEstimate(
            flops=100_000_000_000, bytes_accessed=rows * columns * 8, transcendentals=0
        ),
        name="front",
    )(a, g, f, e)


def finish(a_ref, g_ref, e_ref, q_ref, n_ref, factor_ref, error_ref, update_ref, factor_out):
    tile = error_ref.shape[0]
    at = pl.ds(pl.multiple_of(pl.program_id(0) * tile, tile), tile)
    low_rank = mul(q_ref[...], n_ref[...], TN)
    error_ref[...] = mul(a_ref[:, at], g_ref[...], TN) + e_ref[at, :] - low_rank
    update_ref[...] = low_rank.astype(BF16)
    factor_out[...] = factor_ref[...]


def run_finish(a, g, e, q, n, factor):
    rows, columns = e.shape
    tile = min(512, rows)

    def whole(x):
        return pl.BlockSpec(x.shape, lambda i: (0, 0))

    flat = pl.BlockSpec((tile, columns), lambda i: (i, 0))
    vmem = pl.BlockSpec(memory_space=pltpu.VMEM)
    held = (pltpu.with_memory_space_constraint(x, pltpu.VMEM) for x in (a, g, e))
    return pl.pallas_call(
        finish,
        out_shape=(
            jax.ShapeDtypeStruct(e.shape, F32), jax.ShapeDtypeStruct(e.shape, BF16), jax.ShapeDtypeStruct(factor.shape, F32),
        ),
        grid=(rows // tile,),
        in_specs=[vmem, vmem, vmem, pl.BlockSpec((q.shape[0], tile), lambda i: (0, i)), whole(n), whole(factor)],
        out_specs=(flat, flat, whole(factor)),
        compiler_params=pltpu.CompilerParams(vmem_limit_bytes=VMEM_BYTES),
        name="finish",
    )(*held, q, n, factor)


def solution(mesh):
    sizes = (mesh.shape["replica"], mesh.shape["fsdp"], mesh.shape["tensor"])

    def body(attn_out, out_grad, error_in, factor_in):
        q, factor, n, held, activations, cotangents = run_front(
            sizes, attn_out, out_grad, factor_in.T, error_in[0]
        )
        new_error, update, factor = run_finish(activations, cotangents, held, q, n, factor)
        return new_error[None], update, factor.T

    placed = (
        P(("replica", "tensor"), "fsdp"),
        P(("replica", "fsdp"), "tensor"),
        P("replica", "fsdp", "tensor"),
        P("tensor", None),
    )
    return jax.shard_map(
        body,
        mesh=mesh,
        in_specs=placed,
        out_specs=(P("replica", "fsdp", "tensor"), P("fsdp", "tensor"), P("tensor", None)),
        check_vma=False,
    )
```

```python
import functools

import jax
import jax.numpy as jnp
from jax import lax
from jax.experimental import pallas as pl
from jax.experimental.pallas import tpu as pltpu
from jax.sharding import PartitionSpec as P

MESH = pl.DeviceIdType.MESH
HIGHEST = lax.Precision.HIGHEST
F32, BF16 = jnp.float32, jnp.bfloat16
LANE = 128
NN = (((1,), (0,)), ((), ()))
NT = (((1,), (1,)), ((), ()))
TN = (((0,), (0,)), ((), ()))
VMEM_BYTES = 20 * 1024 * 1024
PIECES = 16
PACE = {
    "start": (2, 1, 0),
    "left1": (2, 0, 0),
    "left2": (1, 1, 1),
    "left3": (1, 1, 2),
    "sum": (1, 1, 1),
    "share": (1, 1, 1),
    "spread": (2, 1, 2),
    "right": (5, 4, 2),
    "factor": (1, 4, 4),
    "return": (0, 2, 3),
    "end": (PIECES, PIECES, PIECES),
}


def mul(a, b, dims=NN, precision=None):
    return lax.dot_general(a, b, dims, precision=precision, preferred_element_type=F32)


def split(x):
    high = x.astype(BF16)
    return high, (x - high.astype(F32)).astype(BF16)


def stacked(x):
    return jnp.concatenate(split(x), axis=0)


def folded(x):
    half = x.shape[0] // 2
    return x[:half] + x[half:]


def slabs(rows):
    width = max(LANE, rows // PIECES)
    return width, rows // width


class Cut:
    def __init__(self, rows, columns, pieces):
        self.down = 1
        while (columns * self.down) % (pieces * LANE) != 0:
            self.down *= 2
        self.across = pieces // self.down
        self.rows, self.columns = rows // self.down, columns // self.across

    def at(self, piece, start=0):
        row = pl.multiple_of((piece // self.across) * self.rows, 8)
        column = pl.multiple_of(start + (piece % self.across) * self.columns, LANE)
        return pl.ds(row, self.rows), pl.ds(column, self.columns)


def inverse_factor(gram):
    rank = gram.shape[0]
    row_at = lax.broadcasted_iota(jnp.int32, (rank, LANE), 0)
    lane_at = lax.broadcasted_iota(jnp.int32, (rank, LANE), 1)
    table = gram + jnp.where(lane_at == row_at + LANE // 2, 1.0, 0.0).astype(F32)
    for k in range(rank):
        row = table[k : k + 1, :]
        inverse = 1.0 / jnp.sqrt(row[:, k : k + 1])
        row = row * inverse
        column = jnp.where(row_at > k, table[:, k : k + 1] * inverse, 0.0)
        table = jnp.where(row_at == k, jnp.broadcast_to(row, table.shape), table - column * row)
    return table[:, LANE // 2 : LANE // 2 + rank]


def front(
    sizes,
    a_ref, g_ref, f_ref, e_ref,
    q_out, n_out, nt_out, e_mem, a_all, g_all,
    q_ref, n_ref, nt_ref,
    f_raw, f_mem, part, left, got_rep, mid, got_ten, gf_out, gf_slots, gram_slots, al_out, al_slots,
    n_part, n_got, n_full,
    e_sem, result_sem, own_sem, out_sem, near_sem, ring_sem, g_sem, gf_sem, rep_sem, ten_sem, ten_back, rep_back, gram_sem, al_sem, n_sem, n_back,
):
    reps, fs, ts = sizes
    r, f, t = lax.axis_index("replica"), lax.axis_index("fsdp"), lax.axis_index("tensor")
    rank, rows = part.shape
    block = rows // reps
    tile = min(512, block)
    per = block // tile
    tok_g, tok_a = g_ref.shape[0], a_ref.shape[0]
    width, pieces = slabs(rows)

    def row_copy(step):
        q = lax.rem(r + 1 + step // per, reps)
        at = pl.ds(pl.multiple_of(q * block + (step % per) * tile, tile), tile)
        return pltpu.make_async_copy(e_ref.at[at], e_mem.at[at], e_sem.at[step])

    plane = [(df, dt) for df in range(fs) for dt in range(ts) if df + dt > 0]
    sheet = [(dr, df) for dr in range(reps) for df in range(fs) if dr + df > 0]

    def in_plane(df, dt):
        return {"replica": r, "fsdp": lax.rem(f + df, fs), "tensor": lax.rem(t + dt, ts)}

    def in_sheet(dr, df):
        return {"replica": lax.rem(r + dr, reps), "fsdp": lax.rem(f + df, fs), "tensor": t}

    barrier = pltpu.get_barrier_semaphore()
    greeted = [in_plane(*d) for d in plane] + [in_sheet(*d) for d in sheet if d[0] > 0]
    for device in greeted:
        pl.semaphore_signal(barrier, inc=1, device_id=device, device_id_type=MESH)

    g_own = pl.ds(pl.multiple_of(f * tok_g, tok_g), tok_g)
    a_own = pl.ds(pl.multiple_of(t * tok_a, tok_a), tok_a)
    own_copies = [
        pltpu.make_async_copy(f_ref, f_raw, own_sem.at[0]),
        pltpu.make_async_copy(g_ref, g_all.at[g_own], own_sem.at[1]),
        pltpu.make_async_copy(a_ref, a_all.at[a_own], own_sem.at[2]),
    ]
    for copy in own_copies:
        copy.start()
    own_copies[0].wait()
    high, low = split(f_raw[...])
    wide = jnp.concatenate(
        [high.astype(F32), low.astype(F32), jnp.zeros((LANE - 2 * rank, f_ref.shape[1]), F32)], axis=0
    )
    f_mem[...] = wide.T.astype(BF16)

    me_plane = f * ts + t
    chunk, a_parts, g_parts = gf_out.shape[2], al_out.shape[0], gf_out.shape[0]

    def meets(f_at, t_at):
        return (t_at // g_parts == f_at) if a_parts == 1 else (f_at // a_parts == t_at)

    own_copies[1].wait()
    own_copies[2].wait()
    for step in range(reps * per):
        row_copy(step).start()
    gf = folded(mul(g_all[g_own, :], f_mem[...]).T[: 2 * rank])
    for j in range(g_parts):
        gf_out[j] = gf[:, j * chunk : (j + 1) * chunk]

    @pl.when(meets(f, t))
    def _():
        gf_slots[me_plane] = gf_out[lax.rem(t, g_parts)]

    pl.semaphore_wait(barrier, len(greeted))

    def spread(source, slots, sems, goes, comes):
        copies = []
        for i, (df, dt) in enumerate(plane):
            to_f, to_t = lax.rem(f + df, fs), lax.rem(t + dt, ts)
            from_f, from_t = lax.rem(f + fs - df, fs), lax.rem(t + ts - dt, ts)
            copy = pltpu.make_async_remote_copy(
                src_ref=source(to_f, to_t), dst_ref=slots.at[me_plane],
                send_sem=sems.at[0, i], recv_sem=sems.at[1, i],
                device_id=in_plane(df, dt), device_id_type=MESH,
            )
            sends = goes(to_f, to_t)
            pl.when(sends)(copy.start)
            copies.append((copy, sends, comes(from_f, from_t)))
        return copies

    def settle(copies):
        for copy, sends, receives in copies:
            pl.when(receives)(copy.wait_recv)
            pl.when(sends)(copy.wait_send)

    gf_copies = spread(
        lambda to_f, to_t: gf_out.at[lax.rem(to_t, g_parts)], gf_slots, gf_sem,
        lambda to_f, to_t: meets(f, to_t), lambda from_f, from_t: meets(from_f, t),
    )

    g_copies = []
    for df in range(1, fs):
        copy = pltpu.make_async_remote_copy(
            src_ref=g_all.at[g_own], dst_ref=g_all.at[g_own],
            send_sem=g_sem.at[0, df - 1], recv_sem=g_sem.at[1, df - 1],
            device_id=in_plane(df, 0), device_id_type=MESH,
        )
        copy.start()
        g_copies.append(copy)


    def part_of(block_at, p):
        return (
            pl.ds(pl.multiple_of(lax.rem(block_at + ts, ts) * tok_a, tok_a), tok_a),
            pl.ds(p * width, width),
        )

    def whole_of(block_at, d):
        return (
            pl.ds(pl.multiple_of(lax.rem(block_at + ts, ts) * tok_a, tok_a), tok_a),
            pl.ds(0, width * direct if d == 1 else rows),
        )

    def inside(x):
        return jnp.logical_and(x >= 0, x < ts)

    direct = pieces - pieces // 8

    def lands_at(way, d, p):
        if d == 1 and p >= direct:
            return ring_sem.at[2 + way, p]
        return ring_sem.at[way, p] if d == 2 else near_sem.at[way, d - 1]

    def bulk(way, d, p):
        sign = 1 - 2 * way
        own = d == 1 or (d == 2 and p < direct)
        block_at = t if own else t - sign * (d - 1)
        dest = t + sign * (d if own else 1)
        at = part_of(block_at, p)
        copy = pltpu.make_async_remote_copy(
            src_ref=a_all.at[at], dst_ref=a_all.at[at],
            send_sem=out_sem.at[way, ts - 1 if d == 2 and not own else d - 1], recv_sem=lands_at(way, d, p),
            device_id={"replica": r, "fsdp": f, "tensor": lax.rem(dest + ts, ts)},
            device_id_type=MESH,
        )
        return copy, jnp.logical_and(inside(block_at), inside(dest))

    def send(d, p):
        if d >= ts:
            return
        for way in range(2):
            copy, valid = bulk(way, d, p)
            pl.when(valid)(copy.start)

    def came(way, d, at, sem):
        copy = pltpu.make_async_remote_copy(
            src_ref=a_all.at[at], dst_ref=a_all.at[at], send_sem=out_sem.at[way, d - 1], recv_sem=sem,
            device_id=in_plane(0, 1), device_id_type=MESH,
        )
        pl.when(inside(t - (1 - 2 * way) * d))(copy.wait_recv)

    landed = set()

    def land(d, p):
        if (d, p) in landed:
            return
        landed.add((d, p))
        for way in range(2):
            came(way, d, part_of(t - (1 - 2 * way) * d, p), lands_at(way, d, p))

    def land_whole(d):
        if d == 2:
            for p in range(pieces):
                land(2, p)
        elif (d, -1) not in landed:
            landed.add((d, -1))
            for way in range(2):
                came(way, d, whole_of(t - (1 - 2 * way) * d, d), near_sem.at[way, d - 1])
            for p in range(direct, pieces if d == 1 else 0):
                land(1, p)

    sent = [0, 0, 0]

    def inject(phase):
        far, near, onward = PACE.get(phase, (0, 0, 0))
        for _ in range(min(far, pieces - sent[0])):
            if sent[0] >= direct and ts > 2:
                land(1, sent[0])
            send(2, sent[0])
            sent[0] += 1
        for _ in range(min(onward, sent[0] - sent[2]) if ts > 3 else 0):
            land(2, sent[2])
            send(3, sent[2])
            sent[2] += 1
        for _ in range(min(near, pieces - sent[1])):
            send(1, (sent[1] + direct) % pieces)
            sent[1] += 1

    inject("start")

    rep_copies = []
    for dr in range(1, reps + 1):
        q = lax.rem(r + dr, reps)
        base = pl.multiple_of(q * block, LANE)
        inject(f"left{dr}")

        def tile_left(j, _, dr=dr, base=base):
            row_copy((dr - 1) * per + j).wait()
            at = pl.ds(pl.multiple_of(base + j * tile, tile), tile)
            eh, el = split(e_mem[at, :])
            total = mul(jnp.concatenate([eh, el], axis=0), f_mem[...])
            total = total[:tile] + total[tile:]
            part[:, at] = folded(total.T[: 2 * rank])
            return 0

        lax.fori_loop(0, per, tile_left, 0)
        if dr == 1:
            settle(gf_copies)
            first = (t * tok_a) // tok_g
            totals = []
            for j in range(a_parts):
                total = gf_slots[(first + j) * ts]
                for dt in range(1, ts):
                    total = total + gf_slots[(first + j) * ts + dt]
                totals.append(total)
            own = stacked(jnp.concatenate(totals, axis=1))
        at = pl.ds(base, block)
        part[:, at] += folded(mul(own, a_all[a_own, at]))
        if dr < reps:
            copy = pltpu.make_async_remote_copy(
                src_ref=part.at[:, at], dst_ref=got_rep.at[dr - 1],
                send_sem=rep_sem.at[0, dr - 1], recv_sem=rep_sem.at[1, dr - 1],
                device_id=in_sheet(dr, 0), device_id_type=MESH,
            )
            copy.start()
            rep_copies.append(copy)

    mine = pl.ds(pl.multiple_of(r * block, LANE), block)
    total = part[:, mine]
    for i, copy in enumerate(rep_copies):
        copy.wait()
        total = total + got_rep[i]
    mid[...] = total

    cut = Cut(rank, block, ts)
    ten_copies = []
    for dt in range(1, ts):
        copy = pltpu.make_async_remote_copy(
            src_ref=mid.at[cut.at(lax.rem(t + dt, ts))], dst_ref=got_ten.at[dt - 1],
            send_sem=ten_sem.at[0, dt - 1], recv_sem=ten_sem.at[1, dt - 1],
            device_id=in_plane(0, dt), device_id_type=MESH,
        )
        copy.start()
        ten_copies.append(copy)
    inject("sum")
    total = mid[cut.at(t)]
    for i, copy in enumerate(ten_copies):
        copy.wait()
        total = total + got_ten[i]
    own = cut.at(t, r * block)
    left[own] = total * (1.0 / reps)
    back = []
    for dt in range(1, ts):
        copy = pltpu.make_async_remote_copy(
            src_ref=left.at[own], dst_ref=left.at[own],
            send_sem=ten_back.at[0, dt - 1], recv_sem=ten_back.at[1, dt - 1],
            device_id=in_plane(0, dt), device_id_type=MESH,
        )
        copy.start()
        back.append(copy)
    inject("share")
    for copy in back:
        copy.wait()
    back = []
    for dr in range(1, reps):
        copy = pltpu.make_async_remote_copy(
            src_ref=left.at[:, mine], dst_ref=left.at[:, mine],
            send_sem=rep_back.at[0, dr - 1], recv_sem=rep_back.at[1, dr - 1],
            device_id=in_sheet(dr, 0), device_id_type=MESH,
        )
        copy.start()
        back.append(copy)
    inject("spread")
    for copy in back:
        copy.wait()

    whole = left[...]
    al = folded(mul(stacked(whole), a_all[a_own, :], NT))
    for j in range(a_parts):
        al_out[j] = al[:, j * chunk : (j + 1) * chunk]

    @pl.when(meets(f, t))
    def _():
        al_slots[me_plane] = al_out[lax.rem(f, a_parts)]

    al_copies = spread(
        lambda to_f, to_t: al_out.at[lax.rem(to_f, a_parts)], al_slots, al_sem,
        lambda to_f, to_t: meets(to_f, t), lambda from_f, from_t: meets(f, from_t),
    )
    inject("right")
    gram_slots[f, :, 0:rank] = mul(whole, whole, NT, HIGHEST)
    gram_slots[f, :, rank:LANE] = jnp.zeros((rank, LANE - rank), F32)
    gram_copies = []
    for df in range(1, fs):
        copy = pltpu.make_async_remote_copy(
            src_ref=gram_slots.at[f], dst_ref=gram_slots.at[f],
            send_sem=gram_sem.at[0, df - 1], recv_sem=gram_sem.at[1, df - 1],
            device_id=in_plane(df, 0), device_id_type=MESH,
        )
        copy.start()
        gram_copies.append(copy)

    n_part[...] = jnp.zeros(n_part.shape, F32)

    def tile_right(j, _):
        at = pl.ds(pl.multiple_of(j * tile, tile), tile)
        eh, el = split(e_mem[at, :])
        both = stacked(left[:, at])
        n_part[...] += folded(mul(jnp.concatenate([both, both], axis=1), jnp.concatenate([eh, el], axis=0)))
        return 0

    lax.fori_loop(0, rows // tile, tile_right, 0)

    settle(al_copies)
    first = (f * tok_g) // tok_a
    totals = []
    for j in range(g_parts):
        total = al_slots[first + j]
        for df in range(1, fs):
            total = total + al_slots[df * ts + first + j]
        totals.append(total)
    tokens = stacked(jnp.concatenate(totals, axis=1))
    n_part[...] += folded(mul(tokens, g_all[g_own, :]))

    n_cut = Cut(rank, n_part.shape[1], reps * fs)
    n_copies = []
    for i, (dr, df) in enumerate(sheet):
        owner = lax.rem(r + dr, reps) * fs + lax.rem(f + df, fs)
        copy = pltpu.make_async_remote_copy(
            src_ref=n_part.at[n_cut.at(owner)], dst_ref=n_got.at[i],
            send_sem=n_sem.at[0, i], recv_sem=n_sem.at[1, i],
            device_id=in_sheet(dr, df), device_id_type=MESH,
        )
        copy.start()
        n_copies.append(copy)

    inject("factor")
    for copy in gram_copies:
        copy.wait()
    gram = gram_slots[0]
    for df in range(1, fs):
        gram = gram + gram_slots[df]
    inverse = inverse_factor(gram)
    high, low = split(mul(inverse, left[...], precision=HIGHEST))
    q_ref[0:rank] = high
    q_ref[rank : 2 * rank] = low
    q_ref[2 * rank :] = high

    place = n_cut.at(r * fs + f)
    total = n_part[place]
    for i, copy in enumerate(n_copies):
        copy.wait()
        total = total + n_got[i]
    n_full[place] = total * (1.0 / reps)
    back = []
    for i, (dr, df) in enumerate(sheet):
        copy = pltpu.make_async_remote_copy(
            src_ref=n_full.at[place], dst_ref=n_full.at[place],
            send_sem=n_back.at[0, i], recv_sem=n_back.at[1, i],
            device_id=in_sheet(dr, df), device_id_type=MESH,
        )
        copy.start()
        back.append(copy)
    inject("return")
    for copy in back:
        copy.wait()
    factor = mul(inverse, n_full[...], precision=HIGHEST)
    n_ref[...] = factor
    high, low = split(factor)
    nt_ref[0:rank] = high
    nt_ref[rank : 2 * rank] = high
    nt_ref[2 * rank :] = low

    out_copies = [
        pltpu.make_async_copy(source, target, result_sem.at[i])
        for i, (source, target) in enumerate(((q_ref, q_out), (n_ref, n_out), (nt_ref, nt_out)))
    ]
    for copy in out_copies:
        copy.start()
    inject("end")
    for copy in out_copies:
        copy.wait()
    for copy in g_copies:
        copy.wait()
    for d in range(4, ts):
        land_whole(d - 1)
        for p in range(pieces):
            send(d, p)
    for d in range(1, ts):
        land_whole(d)
        for way in range(2):
            sign = 1 - 2 * way
            cut = width * direct if d == 2 else 0
            for low, high in ((0, cut), (cut, rows)):
                if high == low:
                    continue
                own = d == 1 or high == cut
                source = t if own else t - sign * (d - 1)
                target = t + sign * (d if own else 1)
                at = (a_own, pl.ds(low, high - low))
                copy = pltpu.make_async_remote_copy(
                    src_ref=a_all.at[at], dst_ref=a_all.at[at],
                    send_sem=out_sem.at[way, ts - 1 if d == 2 and not own else d - 1], recv_sem=near_sem.at[way, d - 1],
                    device_id=in_plane(0, 1), device_id_type=MESH,
                )
                pl.when(jnp.logical_and(inside(source), inside(target)))(copy.wait_send)


def run_front(sizes, a, g, f, e):
    reps, fs, ts = sizes
    rank, rows, columns = f.shape[0], e.shape[0], e.shape[1]
    tok_g, tok_a = g.shape[0], a.shape[0]
    block, chunk = rows // reps, min(tok_a, tok_g)
    cut, n_cut = Cut(rank, block, ts), Cut(rank, columns, reps * fs)
    tiles = rows // min(512, block)
    plane, sheet = fs * ts - 1, reps * fs - 1
    vmem = pl.BlockSpec(memory_space=pltpu.VMEM)
    dma = pltpu.SemaphoreType.DMA
    return pl.pallas_call(
        functools.partial(front, sizes),
        out_shape=(
            jax.ShapeDtypeStruct((3 * rank, rows), BF16),
            jax.ShapeDtypeStruct((rank, columns), F32),
            jax.ShapeDtypeStruct((3 * rank, columns), BF16),
            pltpu.VMEM((rows, columns), F32),
            pltpu.VMEM((tok_a * ts, rows), BF16),
            pltpu.VMEM((tok_g * fs, columns), BF16),
        ),
        in_specs=[pl.BlockSpec(memory_space=pl.ANY)] * 4,
        out_specs=(pl.BlockSpec(memory_space=pl.ANY),) * 3 + (vmem,) * 3,
        scratch_shapes=[
            pltpu.VMEM((3 * rank, rows), BF16),
            pltpu.VMEM((rank, columns), F32),
            pltpu.VMEM((3 * rank, columns), BF16),
            pltpu.VMEM((rank, columns), F32),
            pltpu.VMEM((columns, LANE), BF16),
            pltpu.VMEM((rank, rows), F32),
            pltpu.VMEM((rank, rows), F32),
            pltpu.VMEM((reps - 1, rank, block), F32),
            pltpu.VMEM((rank, block), F32),
            pltpu.VMEM((ts - 1, cut.rows, cut.columns), F32),
            pltpu.VMEM((tok_g // chunk, rank, chunk), F32),
            pltpu.VMEM((fs * ts, rank, chunk), F32),
            pltpu.VMEM((fs, rank, LANE), F32),
            pltpu.VMEM((tok_a // chunk, rank, chunk), F32),
            pltpu.VMEM((fs * ts, rank, chunk), F32),
            pltpu.VMEM((rank, columns), F32),
            pltpu.VMEM((sheet, n_cut.rows, n_cut.columns), F32),
            pltpu.VMEM((rank, columns), F32),
            dma((tiles,)), dma((3,)), dma((3,)), dma((2, ts)), dma((2, ts)), dma((4, PIECES)), dma((2, fs)), dma((2, plane)), dma((2, reps - 1)), dma((2, ts - 1)), dma((2, ts - 1)),
            dma((2, reps - 1)), dma((2, fs)), dma((2, plane)), dma((2, sheet)), dma((2, sheet)),
        ],
        compiler_params=pltpu.CompilerParams(
            collective_id=0, has_side_effects=True, vmem_limit_bytes=VMEM_BYTES
        ),
        cost_estimate=pl.CostEstimate(
            flops=100_000_000_000, bytes_accessed=rows * columns * 8, transcendentals=0
        ),
        name="front",
    )(a, g, f, e)


def finish(a_ref, g_ref, e_ref, q_ref, n_ref, factor_ref, error_ref, update_ref, factor_out):
    tile = error_ref.shape[0]
    at = pl.ds(pl.multiple_of(pl.program_id(0) * tile, tile), tile)
    low_rank = mul(q_ref[...], n_ref[...], TN)
    error_ref[...] = mul(a_ref[:, at], g_ref[...], TN) + e_ref[at, :] - low_rank
    update_ref[...] = low_rank.astype(BF16)
    factor_out[...] = factor_ref[...]


def run_finish(a, g, e, q, n, factor):
    rows, columns = e.shape
    tile = min(512, rows)

    def whole(x):
        return pl.BlockSpec(x.shape, lambda i: (0, 0))

    flat = pl.BlockSpec((tile, columns), lambda i: (i, 0))
    vmem = pl.BlockSpec(memory_space=pltpu.VMEM)
    held = (pltpu.with_memory_space_constraint(x, pltpu.VMEM) for x in (a, g, e))
    return pl.pallas_call(
        finish,
        out_shape=(
            jax.ShapeDtypeStruct(e.shape, F32), jax.ShapeDtypeStruct(e.shape, BF16), jax.ShapeDtypeStruct(factor.shape, F32),
        ),
        grid=(rows // tile,),
        in_specs=[vmem, vmem, vmem, pl.BlockSpec((q.shape[0], tile), lambda i: (0, i)), whole(n), whole(factor)],
        out_specs=(flat, flat, whole(factor)),
        compiler_params=pltpu.CompilerParams(vmem_limit_bytes=VMEM_BYTES),
        name="finish",
    )(*held, q, n, factor)


def solution(mesh):
    sizes = (mesh.shape["replica"], mesh.shape["fsdp"], mesh.shape["tensor"])

    def body(attn_out, out_grad, error_in, factor_in):
        q, factor, n, held, activations, cotangents = run_front(
            sizes, attn_out, out_grad, factor_in.T, error_in[0]
        )
        new_error, update, factor = run_finish(activations, cotangents, held, q, n, factor)
        return new_error[None], update, factor.T

    placed = (
        P(("replica", "tensor"), "fsdp"),
        P(("replica", "fsdp"), "tensor"),
        P("replica", "fsdp", "tensor"),
        P("tensor", None),
    )
    return jax.shard_map(
        body,
        mesh=mesh,
        in_specs=placed,
        out_specs=(P("replica", "fsdp", "tensor"), P("fsdp", "tensor"), P("tensor", None)),
        check_vma=False,
    )
```
